128 devices in a mesh: mp: 8 (over x, z_lo), item: 16 (over z_hi, y, core).
Axes of the slice: x: 4, y: 4, z: 4 (z_hi: 2, z_lo: 2; z = z_hi * 2 + z_lo), core: 2. Of those that a mesh axis runs over, the one named last changes fastest.
Arguments:
- response: int32 [16384, 32768], P('mp', 'item'), may hold values from 0 to 2
- difficulty: float32 [32768], P('item'), may hold values from -4 to 4
- ability: float32 [16384, 256], P('mp', 'item'), may hold values from -6 to 6
- ability_m: float32 [16384, 256], P('mp', 'item'), may hold values from -3 to 3
- ability_v: float32 [16384, 256], P('mp', 'item'), may hold values from 0.02 to 0.5
- discrim: float32 [32768, 256], P('item', 'mp'), may hold values from -0.375 to 0.375
- discrim_m: float32 [32768, 256], P('item', 'mp'), may hold values from -3 to 3
- discrim_v: float32 [32768, 256], P('item', 'mp'), may hold values from 0.02 to 0.5
Outputs:
- ability_new: float32 [16384, 256], P('mp', 'item')
- ability_m_new: float32 [16384, 256], P('mp', 'item')
- ability_v_new: float32 [16384, 256], P('mp', 'item')
- discrim_new: float32 [32768, 256], P('item', 'mp')
- discrim_m_new: float32 [32768, 256], P('item', 'mp')
- discrim_v_new: float32 [32768, 256], P('item', 'mp')
The draws below stay inside these ranges and needn't reach their ends.
Inputs may be any that keep to these rules, and one draw needn't show every extreme that they name: `response`: 0 marks an unobserved pair, 1 an observed wrong answer, 2 an observed right answer.
All inputs are finite; a program needn't handle non-finite values.
Results may differ from the reference program's by a relative error of at most 0.0012.
Values may be sent and summed in bfloat16 or wider, within the bound.
A program may use at most 128 MiB of HBM per device.

```python
import math
import jax
import jax.numpy as jnp
from jax import lax

K = 256
CKPT_DEV = 2048
CKPTS = 16384
ITEMS = 32768
N_MP = 8


def touch_ends(values, own_key, smallest, high):
    shape = values.shape
    spot = [jax.random.randint(jax.random.fold_in(own_key, axis), (), 0, shape[axis]) for axis in range(len(shape))]
    values = values.at[tuple(spot)].set(smallest)
    longest = shape.index(max(shape))
    spot[longest] = (spot[longest] + 1) % shape[longest]
    return values.at[tuple(spot)].set(high)


def block_levels(stream_key, dims, cuts, least, largest):
    gain, own = 1.0, jax.random.fold_in(stream_key, 6)
    for axis_at, parts in cuts:
        draws = jnp.exp(jax.random.uniform(jax.random.fold_in(own, axis_at), (parts,), jnp.float32, least / len(cuts), largest / len(cuts)))
        gain = gain * jnp.repeat(draws, dims[axis_at] // parts).reshape([-1 if axis == axis_at else 1 for axis in range(len(dims))])
    return gain


def bell_draw(key, shape, scale, reach, shards=(), kind=jnp.bfloat16):
    array = jax.random.normal(key, shape, jnp.float32) * scale
    if len(shards) > 0:
        array = block_levels(key, shape, shards, -0.22, 0.18) * array
    return jnp.clip(array, min=-reach, max=reach).astype(kind)


def setup_inputs(seed: int = 0) -> dict:
    keys = jax.random.split(jax.random.key(seed), 9)
    response = touch_ends(jax.random.randint(keys[0], (CKPTS, ITEMS), 0, 3), jax.random.fold_in(keys[0], 1), 0, 2).astype(jnp.int32)
    difficulty = bell_draw(keys[1], (ITEMS,), 1.0, 4.0, ((0, 16),), jnp.float32)
    ability = bell_draw(keys[2], (CKPTS, K), 1.0, 6.0, ((0, 8), (1, 16)), jnp.float32)
    ability_m = bell_draw(keys[3], (CKPTS, K), 0.4, 3.0, ((0, 8), (1, 16)), jnp.float32)
    ability_v = jnp.clip(jnp.exp(math.log(0.5) - 3.218876 * jax.random.uniform(keys[4], (CKPTS, K), jnp.float32) ** block_levels(keys[4], (CKPTS, K), ((0, 8), (1, 16)), -0.2, 0.2)), 0.02, 0.5)
    discrim = bell_draw(keys[5], (ITEMS, K), K ** -0.5, 0.375, ((0, 16), (1, 8)), jnp.float32)
    discrim_m = bell_draw(keys[6], (ITEMS, K), 0.4, 3.0, ((0, 16), (1, 8)), jnp.float32)
    discrim_v = jnp.clip(jnp.exp(math.log(0.5) - 3.218876 * jax.random.uniform(keys[7], (ITEMS, K), jnp.float32) ** block_levels(keys[7], (ITEMS, K), ((0, 16), (1, 8)), -0.2, 0.2)), 0.02, 0.5)
    return dict(response=response, difficulty=difficulty, ability=ability, ability_m=ability_m, ability_v=ability_v, discrim=discrim, discrim_m=discrim_m, discrim_v=discrim_v)


beta_one = 0.9
beta_two = 0.999
corr_one = 1.0 - 0.9 ** 10
corr_two = 1.0 - 0.999 ** 10
adam_eps = 1e-08

def adam_update(factor, moment, second, gradient, step_rate):
    moment_new = beta_one * moment + (1.0 - beta_one) * gradient
    second_new = beta_two * second + (1.0 - beta_two) * gradient * gradient
    update = moment_new / corr_one / (jnp.sqrt(second_new / corr_two) + adam_eps)
    return (factor - step_rate * update, moment_new, second_new)

def reference(response, difficulty, ability, ability_m, ability_v, discrim, discrim_m, discrim_v):
    ability_bf = ability.astype(jnp.bfloat16)
    discrim_bf = discrim.astype(jnp.bfloat16)
    discrim_wide = discrim_bf.astype(jnp.float32)
    ability_blocks = ability_bf.reshape(N_MP, CKPT_DEV, K)
    response_blocks = response.reshape(N_MP, CKPT_DEV, ITEMS)

    def block_step(total, pieces):
        rows_bf, rows_response = pieces
        logits = jnp.dot(rows_bf, discrim_bf.T, preferred_element_type=jnp.float32) + difficulty[None, :]
        correct = (rows_response == 2).astype(jnp.float32)
        residual = jnp.where(rows_response > 0, jax.nn.sigmoid(logits) - correct, jnp.float32(0.0))
        grad_rows = jnp.dot(residual, discrim_wide, precision=lax.Precision.HIGHEST)
        total = total + jnp.dot(residual.T, rows_bf.astype(jnp.float32), precision=lax.Precision.HIGHEST)
        return (total, grad_rows)
    start_total = jnp.zeros((ITEMS, K), jnp.float32)
    discrim_sum, ability_rows = lax.scan(block_step, start_total, (ability_blocks, response_blocks))
    ability_grad = ability_rows.reshape(CKPTS, K) * math.sqrt(K / ITEMS)
    discrim_grad = discrim_sum * math.sqrt(1.0 / CKPTS)
    ability_new, ability_m_new, ability_v_new = adam_update(ability, ability_m, ability_v, ability_grad, 0.05)
    discrim_new, discrim_m_new, discrim_v_new = adam_update(discrim, discrim_m, discrim_v, discrim_grad, 0.01)
    return (ability_new, ability_m_new, ability_v_new, discrim_new, discrim_m_new, discrim_v_new)
```

```python
import math

import jax
import jax.numpy as jnp
from jax import lax
from jax.experimental import pallas as pl
from jax.experimental.pallas import tpu as pltpu
from jax.sharding import PartitionSpec as P

K = 256
N = 2048
RH, CJ = 1024, 512
NR, NJ = N // RH, N // CJ
RING = 4
DB, AB = 32, 16

TILES = ((0, 0), (1, 0), (0, 1), (1, 1), (2, 0), (3, 0), (2, 1), (3, 1))

D_MSG, A_MSG, C_MSG, RD_MSG, RA_MSG = 8, 9, 8, 8, 9
BASE_D = 0
BASE_A = BASE_D + NJ * D_MSG
BASE_C = BASE_A + NR * A_MSG
BASE_RD = BASE_C + NR * C_MSG
BASE_RA = BASE_RD + NJ * RD_MSG
BASE_RC = BASE_RA + NR * RA_MSG
N_SEM = BASE_RC + NR

beta_one = 0.9
beta_two = 0.999
corr_one = 1.0 - 0.9**10
corr_two = 1.0 - 0.999**10
adam_eps = 1e-08

BF = jnp.bfloat16
F32 = jnp.float32


def adam_update(factor, moment, second, gradient, step_rate):
    moment_new = beta_one * moment + (1.0 - beta_one) * gradient
    second_new = beta_two * second + (1.0 - beta_two) * gradient * gradient
    update = moment_new / corr_one / (jnp.sqrt(second_new / corr_two) + adam_eps)
    return (factor - step_rate * update, moment_new, second_new)


def kernel(
    ability_ref, discrim_ref, diff_ref, resp_ref, ga_out, gd_out,
    at, asc, dt, rv, ga, gd, rb, sd, rd, sa, ra, cs, cr,
    send_sem, recv_sem, resp_sem,
):
    mp, item = lax.axis_index("mp"), lax.axis_index("item")
    x, p = mp // 2, mp % 2
    z, y, c = item // 8, (item // 2) % RING, item % 2

    def mp_dev(dx, flip):
        return {"mp": ((x + dx) % RING) * 2 + (1 - p if flip else p)}

    def item_dev(dy, flip):
        return {"item": ((1 - z if flip else z) * RING + (y + dy) % RING) * 2 + c}

    x_next, x_prev, x_pair = mp_dev(1, False), mp_dev(RING - 1, False), mp_dev(0, True)
    y_next, y_prev, y_pair = item_dev(1, False), item_dev(RING - 1, False), item_dev(0, True)
    core = {"item": item + 1 - 2 * c}

    sent = []

    def message(index, src, dst, device):
        return pltpu.make_async_remote_copy(
            src_ref=src, dst_ref=dst, send_sem=send_sem.at[index], recv_sem=recv_sem.at[index],
            device_id=device, device_id_type=pl.DeviceIdType.MESH,
        )

    landed = {}

    def send(index, src, dst, device):
        copy = message(index, src, dst, device)
        copy.start()
        sent.append(copy)
        landed[index] = copy

    def arrive(index):
        landed[index].wait_recv()

    def d_rows(dx, flip):
        block = ((x + dx) % RING) * 2 + (1 - p if flip else p)
        return pl.multiple_of(block * DB, DB)

    def d_block(j, dx, flip):
        return dt.at[j, pl.ds(d_rows(dx, flip), DB), :]

    def d_half(j, dx, flip, half):
        return dt.at[j, pl.ds(pl.multiple_of(d_rows(dx, flip) + half * (DB // 2), DB // 2), DB // 2), :]

    def d_send(j, m, ref, device):
        send(BASE_D + j * D_MSG + m, ref, ref, device)

    def d_wait(j, m):
        arrive(BASE_D + j * D_MSG + m)

    def d_step0(j):
        own = d_block(j, 0, False)
        d_send(j, 0, own, x_pair)
        d_send(j, 1, own, x_next)
        d_send(j, 2, own, x_prev)

    def d_step1(j):
        d_wait(j, 0)
        other = d_block(j, 0, True)
        d_send(j, 3, other, x_next)
        d_send(j, 4, other, x_prev)
        d_wait(j, 1)
        d_send(j, 5, d_half(j, RING - 1, False, 0), x_next)
        d_wait(j, 2)
        d_send(j, 6, d_half(j, 1, False, 1), x_prev)

    def d_step2(j):
        d_wait(j, 5)
        d_wait(j, 6)
        d_send(j, 7, d_block(j, 2, False), x_pair)

    def d_done(j):
        d_wait(j, 3)
        d_wait(j, 4)
        d_wait(j, 7)

    def a_rows(dy, flip, which):
        chip = (1 - z if flip else z) * RING + (y + dy) % RING
        return pl.multiple_of((chip * 2 + which) * AB, AB)

    def a_block(r, dy, flip):
        return at.at[r, pl.ds(a_rows(dy, flip, c), AB), :]

    def a_half(r, dy, flip, half):
        return at.at[r, pl.ds(a_rows(dy, flip, c), AB), half * (RH // 2) : (half + 1) * (RH // 2)]

    def a_send(r, m, ref, device):
        send(BASE_A + r * A_MSG + m, ref, ref, device)

    def a_wait(r, m):
        arrive(BASE_A + r * A_MSG + m)

    def c_send(r, m, ref):
        send(BASE_C + r * C_MSG + m, ref, ref, core)

    def a_step0(r):
        own = a_block(r, 0, False)
        a_send(r, 0, own, y_pair)
        a_send(r, 1, own, y_next)
        a_send(r, 2, own, y_prev)
        c_send(r, 0, own)

    def a_step1(r):
        a_wait(r, 1)
        a_send(r, 5, a_half(r, RING - 1, False, 0), y_next)
        a_wait(r, 2)
        a_send(r, 6, a_half(r, 1, False, 1), y_prev)
        c_send(r, 2, a_block(r, RING - 1, False))
        c_send(r, 3, a_block(r, 1, False))
        a_wait(r, 0)
        other = a_block(r, 0, True)
        a_send(r, 3, other, y_next)
        a_send(r, 4, other, y_prev)
        c_send(r, 1, other)

    def a_step2(r):
        a_wait(r, 3)
        a_send(r, 7, a_half(r, RING - 1, True, 0), y_next)
        a_wait(r, 4)
        a_send(r, 8, a_half(r, 1, True, 1), y_prev)
        c_send(r, 4, a_block(r, RING - 1, True))
        c_send(r, 5, a_block(r, 1, True))

    def a_step3(r):
        a_wait(r, 5)
        a_wait(r, 6)
        c_send(r, 6, a_block(r, 2, False))
        a_wait(r, 7)
        a_wait(r, 8)
        c_send(r, 7, a_block(r, 2, True))

    def a_done(r):
        for m in range(C_MSG):
            arrive(BASE_C + r * C_MSG + m)
        for i in range(RH // 512):
            part = at[r, :, i * 512 : (i + 1) * 512].astype(F32) * 0.5
            asc[r, i * 512 : (i + 1) * 512, :] = part.T.astype(BF)

    def rd_send(j, m, value, device):
        sd[j, m] = value.astype(BF)
        send(BASE_RD + j * RD_MSG + m, sd.at[j, m], rd.at[j, m], device)

    def rd_send_half(j, m, value, device):
        sd[j, m, 0 : DB // 2] = value.astype(BF)
        send(
            BASE_RD + j * RD_MSG + m, sd.at[j, m, pl.ds(0, DB // 2)], rd.at[j, m, pl.ds(0, DB // 2)], device
        )

    def rd_wait(j, m):
        arrive(BASE_RD + j * RD_MSG + m)

    def d_part(j, dx, flip):
        return gd[j, pl.ds(d_rows(dx, flip), DB), :]

    def rd_step1(j):
        rd_send(j, 1, d_part(j, 1, True), x_next)
        rd_send(j, 2, d_part(j, RING - 1, True), x_prev)
        rd_send(j, 0, d_part(j, 2, True), x_pair)

    def rd_step2(j):
        rd_wait(j, 0)
        far = d_part(j, 2, False) + rd[j, 0].astype(F32)
        rd_send_half(j, 3, far[: DB // 2], x_next)
        rd_send_half(j, 4, far[DB // 2 :], x_prev)
        rd_wait(j, 1)
        rd_wait(j, 2)
        rd_send(j, 5, d_part(j, 0, True) + rd[j, 1].astype(F32) + rd[j, 2].astype(F32), x_pair)

    def rd_step3(j):
        rd_wait(j, 3)
        near = d_part(j, 1, False)
        rd_send(
            j, 6,
            jnp.concatenate([near[: DB // 2] + rd[j, 3, 0 : DB // 2].astype(F32), near[DB // 2 :]], axis=0),
            x_next,
        )
        rd_wait(j, 4)
        near = d_part(j, RING - 1, False)
        rd_send(
            j, 7,
            jnp.concatenate([near[: DB // 2], near[DB // 2 :] + rd[j, 4, 0 : DB // 2].astype(F32)], axis=0),
            x_prev,
        )

    d_scale = 0.5 * math.sqrt(1.0 / 16384)
    a_scale = 0.5 * math.sqrt(K / 32768)

    def rd_final(j):
        for m in (5, 6, 7):
            rd_wait(j, m)
        total = d_part(j, 0, False) + rd[j, 5].astype(F32) + rd[j, 6].astype(F32) + rd[j, 7].astype(F32)
        gd_out[:, j * CJ : (j + 1) * CJ] = total * d_scale

    H = RH // 2

    def ra_core(r):
        for b in range(8):
            rows = pl.ds(pl.multiple_of(b * 2 * AB + (1 - c) * AB, AB), AB)
            cs[r, b] = ga[r, rows, :].astype(BF)
        send(BASE_RC + r, cs.at[r], cr.at[r], core)

    def a_part(r, dy, flip, half):
        return ga[r, pl.ds(a_rows(dy, flip, c), AB), half * H : (half + 1) * H]

    def ra_start(r, m, halves, device):
        lo, n = halves
        ref = lambda buf: buf.at[r, m, pl.ds(lo, n)]
        send(BASE_RA + r * RA_MSG + m, ref(sa), ref(ra), device)

    def ra_half(r, m, half, value, device):
        sa[r, m, half] = value.astype(BF)
        ra_start(r, m, (half, 1), device)

    def ra_full(r, m, values, device):
        for half in range(2):
            sa[r, m, half] = values[half].astype(BF)
        ra_start(r, m, (0, 2), device)

    def ra_wait(r, m):
        arrive(BASE_RA + r * RA_MSG + m)

    def ra_step1(r):
        arrive(BASE_RC + r)
        for b in range(8):
            rows = pl.ds(pl.multiple_of(b * 2 * AB + c * AB, AB), AB)
            ga[r, rows, :] += cr[r, b].astype(F32)
        ra_half(r, 0, 0, a_part(r, 2, True, 0), y_next)
        ra_half(r, 1, 1, a_part(r, 2, True, 1), y_prev)
        ra_half(r, 2, 0, a_part(r, 2, False, 0), y_next)
        ra_half(r, 3, 1, a_part(r, 2, False, 1), y_prev)

    def ra_step2(r):
        for first, flip in ((0, True), (2, False)):
            ra_wait(r, first)
            ra_full(
                r, 4 + first,
                (a_part(r, 1, flip, 0) + ra[r, first, 0].astype(F32), a_part(r, 1, flip, 1)), y_next,
            )
            ra_wait(r, first + 1)
            ra_full(
                r, 5 + first,
                (a_part(r, RING - 1, flip, 0), a_part(r, RING - 1, flip, 1) + ra[r, first + 1, 1].astype(F32)),
                y_prev,
            )

    def ra_step3(r):
        ra_wait(r, 4)
        ra_wait(r, 5)
        ra_full(
            r, 8,
            [a_part(r, 0, True, h) + ra[r, 4, h].astype(F32) + ra[r, 5, h].astype(F32) for h in range(2)],
            y_pair,
        )

    def ra_final(r):
        for m in (6, 7, 8):
            ra_wait(r, m)
        for h in range(2):
            total = a_part(r, 0, False, h)
            for m in (6, 7, 8):
                total = total + ra[r, m, h].astype(F32)
            ga_out[:, r * RH + h * H : r * RH + (h + 1) * H] = total * a_scale

    def resp_copy(j, r):
        return pltpu.make_async_copy(
            resp_ref.at[r * RH : (r + 1) * RH, j * CJ : (j + 1) * CJ], rv.at[j, r], resp_sem.at[j * NR + r]
        )

    def front(t):
        j, r = TILES[t]
        resp_copy(j, r).wait()
        logits = jnp.dot(asc[r], dt[j], preferred_element_type=F32) + diff_ref[:, j * CJ : (j + 1) * CJ] * 0.5
        score = rv[j, r]
        sign = jnp.where(score == 2, -1.0, 1.0)
        rb[t % 2] = jnp.where(score > 0, jnp.tanh(logits) + sign, 0.0).astype(BF)

    seen_j, seen_r = set(), set()

    def back(t):
        j, r = TILES[t]
        residual = rb[t % 2]
        part_a = lax.dot_general(dt[j], residual, (((1,), (1,)), ((), ())), preferred_element_type=F32)
        part_d = jnp.dot(at[r], residual, preferred_element_type=F32)
        if r in seen_r:
            ga[r] += part_a
        else:
            ga[r] = part_a
        if j in seen_j:
            gd[j] += part_d
        else:
            gd[j] = part_d
        seen_r.add(r)
        seen_j.add(j)

    for j, r in TILES:
        resp_copy(j, r).start()
    for r in range(NR):
        at[r, pl.ds(a_rows(0, False, c), AB), :] = ability_ref[:, r * RH : (r + 1) * RH].astype(BF)
    for j in range(NJ):
        dt[j, pl.ds(d_rows(0, False), DB), :] = discrim_ref[:, j * CJ : (j + 1) * CJ].astype(BF)

    barrier = pltpu.get_barrier_semaphore()
    neighbours = (x_next, x_prev, x_pair, y_next, y_prev, y_pair, core)
    for device in neighbours:
        pl.semaphore_signal(barrier, inc=1, device_id=device, device_id_type=pl.DeviceIdType.MESH)
    pl.semaphore_wait(barrier, len(neighbours))

    a_step0(0)
    d_step0(0)
    d_step0(1)
    a_step0(1)
    d_step1(0)
    a_step1(0)
    d_step2(0)
    a_step2(0)
    d_step1(1)
    d_step0(2)
    a_step3(0)
    a_step1(1)
    d_step2(1)
    a_done(0)
    d_done(0)
    a_step2(1)
    front(0)
    d_done(1)
    front(1)
    back(0)
    a_step3(1)
    d_step1(2)
    d_step0(3)
    a_done(1)
    front(2)
    back(1)
    d_step2(2)
    d_step1(3)
    front(3)
    back(2)
    rd_step1(0)
    d_done(2)
    d_step2(3)
    front(4)
    back(3)
    rd_step1(1)
    rd_step2(0)
    d_done(3)
    front(5)
    back(4)
    rd_step3(0)
    rd_step2(1)
    front(6)
    back(5)
    ra_core(0)
    rd_step3(1)
    rd_final(0)
    front(7)
    back(6)
    rd_step1(2)
    ra_step1(0)
    rd_final(1)
    back(7)
    ra_core(1)
    rd_step1(3)
    rd_step2(2)
    ra_step2(0)
    ra_step1(1)
    rd_step2(3)
    rd_step3(2)
    ra_step3(0)
    ra_step2(1)
    rd_step3(3)
    ra_step3(1)
    rd_final(2)
    ra_final(0)
    rd_final(3)
    ra_final(1)
    for copy in sent:
        copy.wait_send()


def shards(response, difficulty, ability, ability_m, ability_v, discrim, discrim_m, discrim_v):
    vmem = pl.BlockSpec(memory_space=pltpu.VMEM)
    ga_t, gd_t = pl.pallas_call(
        kernel,
        out_shape=(jax.ShapeDtypeStruct((AB, N), F32), jax.ShapeDtypeStruct((DB, N), F32)),
        in_specs=[vmem, vmem, vmem, pl.BlockSpec(memory_space=pl.ANY)],
        out_specs=(vmem, vmem),
        scratch_shapes=[
            pltpu.VMEM((NR, K, RH), BF),
            pltpu.VMEM((NR, RH, K), BF),
            pltpu.VMEM((NJ, K, CJ), BF),
            pltpu.VMEM((NJ, NR, RH, CJ), jnp.int32),
            pltpu.VMEM((NR, K, RH), F32),
            pltpu.VMEM((NJ, K, CJ), F32),
            pltpu.VMEM((2, RH, CJ), BF),
            pltpu.VMEM((NJ, RD_MSG, DB, CJ), BF),
            pltpu.VMEM((NJ, RD_MSG, DB, CJ), BF),
            pltpu.VMEM((NR, RA_MSG, 2, AB, RH // 2), BF),
            pltpu.VMEM((NR, RA_MSG, 2, AB, RH // 2), BF),
            pltpu.VMEM((NR, 8, AB, RH), BF),
            pltpu.VMEM((NR, 8, AB, RH), BF),
            pltpu.SemaphoreType.DMA((N_SEM,)),
            pltpu.SemaphoreType.DMA((N_SEM,)),
            pltpu.SemaphoreType.DMA((NJ * NR,)),
        ],
        compiler_params=pltpu.CompilerParams(
            collective_id=0, has_side_effects=True, vmem_limit_bytes=60 << 20
        ),
        name="irt_step",
    )(ability.T, discrim.T, difficulty[None, :], response)
    ability_new, ability_m_new, ability_v_new = adam_update(ability, ability_m, ability_v, ga_t.T, 0.05)
    discrim_new, discrim_m_new, discrim_v_new = adam_update(discrim, discrim_m, discrim_v, gd_t.T, 0.01)
    return (ability_new, ability_m_new, ability_v_new, discrim_new, discrim_m_new, discrim_v_new)


def solution(mesh):
    return jax.shard_map(
        shards,
        mesh=mesh,
        in_specs=(
            P("mp", "item"),
            P("item"),
            P("mp", "item"),
            P("mp", "item"),
            P("mp", "item"),
            P("item", "mp"),
            P("item", "mp"),
            P("item", "mp"),
        ),
        out_specs=(
            P("mp", "item"),
            P("mp", "item"),
            P("mp", "item"),
            P("item", "mp"),
            P("item", "mp"),
            P("item", "mp"),
        ),
        check_vma=False,
    )
```

```python
import math

import jax
import jax.numpy as jnp
from jax import lax
from jax.experimental import pallas as pl
from jax.experimental.pallas import tpu as pltpu
from jax.sharding import PartitionSpec as P

K = 256
N = 2048
RH, CJ = 1024, 512
NR, NJ = N // RH, N // CJ
RING = 4
DB, AB = 32, 16
ROW = CJ * 4
BLOCK = DB * CJ * 2

TILES = ((0, 0), (1, 0), (0, 1), (1, 1), (2, 0), (3, 0), (2, 1), (3, 1))

G_D, G_A, S_D, S_A = 0, 3 * NJ, 3 * NJ + 3 * NR, 6 * NJ + 3 * NR
N_SEM = 6 * NJ + 6 * NR

beta_one = 0.9
beta_two = 0.999
corr_one = 1.0 - 0.9**10
corr_two = 1.0 - 0.999**10
adam_eps = 1e-08

BF = jnp.bfloat16
F32 = jnp.float32


def adam_update(factor, moment, second, gradient, step_rate):
    moment_new = beta_one * moment + (1.0 - beta_one) * gradient
    second_new = beta_two * second + (1.0 - beta_two) * gradient * gradient
    update = moment_new / corr_one / (jnp.sqrt(second_new / corr_two) + adam_eps)
    return (factor - step_rate * update, moment_new, second_new)


def kernel(
    ability_ref, discrim_ref, diff_ref, resp_ref, ga_out, gd_out,
    at, asc, dt, rv, ga, gd, rb, sd, rd, sa, ra, cs, cr,
    send_sem, recv_sem, resp_sem,
):
    mp, item = lax.axis_index("mp"), lax.axis_index("item")
    x, p = mp // 2, mp % 2
    z, y, c = item // 8, (item // 2) % RING, item % 2

    def mp_dev(dx, flip):
        return {"mp": ((x + dx) % RING) * 2 + (1 - p if flip else p)}

    def item_dev(dy, flip):
        return {"item": ((1 - z if flip else z) * RING + (y + dy) % RING) * 2 + c}

    xs = {d: mp_dev(d, False) for d in (1, 2, 3)}
    ys = {d: item_dev(d, False) for d in (1, 2, 3)}
    x_pair, y_pair = mp_dev(0, True), item_dev(0, True)
    core = {"item": item + 1 - 2 * c}

    sent_rows = [0, 0]

    def send(phase, index, src, dst, device):
        pltpu.make_async_remote_copy(
            src_ref=src, dst_ref=dst, send_sem=send_sem.at[phase], recv_sem=recv_sem.at[index],
            device_id=device, device_id_type=pl.DeviceIdType.MESH,
        ).start()
        sent_rows[phase] += math.prod(src.shape) * 2 // ROW

    def wait_rows(sem, rows):
        ref = rv.at[0, 0, pl.ds(0, rows)]
        pltpu.make_async_copy(ref, ref, sem).wait()

    def arrive(index, blocks):
        wait_rows(recv_sem.at[index], blocks * BLOCK // ROW)

    def d_rows(dx, flip):
        block = ((x + dx) % RING) * 2 + (1 - p if flip else p)
        return pl.multiple_of(block * DB, DB)

    def d_send(j, s, dx, flip, device):
        ref = dt.at[j, pl.ds(d_rows(dx, flip), DB), :]
        send(0, G_D + 3 * j + s, ref, ref, device)

    def d_step0(j):
        d_send(j, 0, 0, False, x_pair)
        d_send(j, 1, 0, False, xs[2])
        d_send(j, 2, 0, False, xs[1])
        d_send(j, 2, 0, False, xs[3])

    def d_step1(j):
        arrive(G_D + 3 * j, 1)
        d_send(j, 2, 0, True, xs[1])
        d_send(j, 2, 0, True, xs[3])

    def d_step2(j):
        arrive(G_D + 3 * j + 1, 1)
        d_send(j, 2, 2, False, x_pair)

    def d_done(j):
        arrive(G_D + 3 * j + 2, 5)

    def a_chip(dy, flip):
        return (1 - z if flip else z) * RING + (y + dy) % RING

    def a_send(r, s, dy, flip, device):
        ref = at.at[r, a_chip(dy, flip), c]
        send(0, G_A + 3 * r + s, ref, ref, device)

    def a_step0(r):
        a_send(r, 0, 0, False, y_pair)
        for d in (2, 1, 3):
            a_send(r, 1, 0, False, ys[d])

    def a_step1(r):
        arrive(G_A + 3 * r, 1)
        for d in (2, 1, 3):
            a_send(r, 1, 0, True, ys[d])

    def a_step2(r):
        arrive(G_A + 3 * r + 1, 6)
        ref = at.at[r, :, c]
        send(0, G_A + 3 * r + 2, ref, ref, core)

    def a_done(r):
        arrive(G_A + 3 * r + 2, 8)
        for i in range(RH // 512):
            part = at[r, :, :, :, i * 512 : (i + 1) * 512].reshape(K, 512).astype(F32) * 0.5
            asc[r, i * 512 : (i + 1) * 512, :] = part.T.astype(BF)

    def rd_send(j, m, s, value, device):
        sd[j, m] = value.astype(BF)
        send(1, S_D + 3 * j + s, sd.at[j, m], rd.at[j, m], device)

    def d_part(j, dx, flip):
        return gd[j, pl.ds(d_rows(dx, flip), DB), :]

    def d_in(j, m):
        return rd[j, m].astype(F32)

    def rd_step1(j):
        rd_send(j, 0, 0, d_part(j, 1, True), xs[1])
        rd_send(j, 1, 0, d_part(j, 3, True), xs[3])
        rd_send(j, 2, 1, d_part(j, 2, True), x_pair)
        rd_send(j, 3, 2, d_part(j, 1, False), xs[1])
        rd_send(j, 4, 2, d_part(j, 3, False), xs[3])

    def rd_step2(j):
        arrive(S_D + 3 * j + 1, 1)
        rd_send(j, 6, 2, d_part(j, 2, False) + d_in(j, 2), xs[2])
        arrive(S_D + 3 * j, 2)
        rd_send(j, 5, 2, d_part(j, 0, True) + d_in(j, 0) + d_in(j, 1), x_pair)

    d_scale = 0.5 * math.sqrt(1.0 / 16384)
    a_scale = 0.5 * math.sqrt(K / 32768)

    def rd_final(j):
        arrive(S_D + 3 * j + 2, 4)
        total = d_part(j, 0, False)
        for m in (3, 4, 5, 6):
            total = total + d_in(j, m)
        gd_out[:, j * CJ : (j + 1) * CJ] = total * d_scale

    def a_rows(chip, which):
        return pl.ds(pl.multiple_of((chip * 2 + which) * AB, AB), AB)

    def ra_core(r):
        for b in range(8):
            cs[r, b] = ga[r, a_rows(b, 1 - c), :].astype(BF)
        send(1, S_A + 3 * r, cs.at[r], cr.at[r], core)

    def a_part(r, dy, flip):
        chip = a_chip(dy, flip)
        return ga[r, a_rows(chip, c), :] + cr[r, chip].astype(F32)

    def ra_send(r, m, s, value, device):
        sa[r, m] = value.astype(BF)
        send(1, S_A + 3 * r + s, sa.at[r, m], ra.at[r, m], device)

    def ra_step1(r):
        arrive(S_A + 3 * r, 8)
        for d in (2, 1, 3):
            ra_send(r, d - 1, 1, a_part(r, d, True), ys[d])
        for d in (2, 1, 3):
            ra_send(r, d + 2, 2, a_part(r, d, False), ys[d])

    def ra_step2(r):
        arrive(S_A + 3 * r + 1, 3)
        total = a_part(r, 0, True)
        for m in (0, 1, 2):
            total = total + ra[r, m].astype(F32)
        ra_send(r, 6, 2, total, y_pair)

    def ra_final(r):
        arrive(S_A + 3 * r + 2, 4)
        total = a_part(r, 0, False)
        for m in (3, 4, 5, 6):
            total = total + ra[r, m].astype(F32)
        ga_out[:, r * RH : (r + 1) * RH] = total * a_scale

    def resp_copy(j, r):
        return pltpu.make_async_copy(
            resp_ref.at[r * RH : (r + 1) * RH, j * CJ : (j + 1) * CJ], rv.at[j, r], resp_sem.at[j * NR + r]
        )

    def front(t):
        j, r = TILES[t]
        resp_copy(j, r).wait()
        logits = jnp.dot(asc[r], dt[j], preferred_element_type=F32) + diff_ref[:, j * CJ : (j + 1) * CJ] * 0.5
        score = rv[j, r]
        sign = jnp.where(score == 2, -1.0, 1.0)
        rb[t % 2] = jnp.where(score > 0, jnp.tanh(logits) + sign, 0.0).astype(BF)

    seen_j, seen_r = set(), set()

    def back(t):
        j, r = TILES[t]
        residual = rb[t % 2]
        part_a = lax.dot_general(dt[j], residual, (((1,), (1,)), ((), ())), preferred_element_type=F32)
        part_d = jnp.dot(at[r].reshape(K, RH), residual, preferred_element_type=F32)
        if r in seen_r:
            ga[r] += part_a
        else:
            ga[r] = part_a
        if j in seen_j:
            gd[j] += part_d
        else:
            gd[j] = part_d
        seen_r.add(r)
        seen_j.add(j)

    for j, r in TILES:
        resp_copy(j, r).start()
    for r in range(NR):
        at[r, a_chip(0, False), c] = ability_ref[:, r * RH : (r + 1) * RH].astype(BF)
    for j in range(NJ):
        dt[j, pl.ds(d_rows(0, False), DB), :] = discrim_ref[:, j * CJ : (j + 1) * CJ].astype(BF)

    barrier = pltpu.get_barrier_semaphore()
    neighbours = (*xs.values(), x_pair, *ys.values(), y_pair, core)
    for device in neighbours:
        pl.semaphore_signal(barrier, inc=1, device_id=device, device_id_type=pl.DeviceIdType.MESH)
    pl.semaphore_wait(barrier, len(neighbours))

    a_step0(0)
    d_step0(0)
    d_step0(1)
    a_step0(1)
    d_step1(0)
    a_step1(0)
    d_step2(0)
    d_step0(2)
    d_step1(1)
    a_step1(1)
    d_step2(1)
    a_step2(0)
    d_step0(3)
    a_done(0)
    d_done(0)
    front(0)
    d_done(1)
    front(1)
    back(0)
    a_step2(1)
    d_step1(2)
    d_step2(2)
    a_done(1)
    front(2)
    back(1)
    d_step1(3)
    d_step2(3)
    front(3)
    back(2)
    rd_step1(0)
    d_done(2)
    front(4)
    back(3)
    rd_step1(1)
    rd_step2(0)
    d_done(3)
    front(5)
    back(4)
    rd_step2(1)
    front(6)
    back(5)
    ra_core(0)
    rd_final(0)
    front(7)
    back(6)
    rd_step1(2)
    ra_step1(0)
    rd_final(1)
    back(7)
    ra_core(1)
    rd_step1(3)
    rd_step2(2)
    ra_step1(1)
    ra_step2(0)
    rd_step2(3)
    ra_step2(1)
    rd_final(2)
    ra_final(0)
    rd_final(3)
    ra_final(1)
    for phase in range(2):
        wait_rows(send_sem.at[phase], sent_rows[phase])


def shards(response, difficulty, ability, ability_m, ability_v, discrim, discrim_m, discrim_v):
    vmem = pl.BlockSpec(memory_space=pltpu.VMEM)
    ga_t, gd_t = pl.pallas_call(
        kernel,
        out_shape=(jax.ShapeDtypeStruct((AB, N), F32), jax.ShapeDtypeStruct((DB, N), F32)),
        in_specs=[vmem, vmem, vmem, pl.BlockSpec(memory_space=pl.ANY)],
        out_specs=(vmem, vmem),
        scratch_shapes=[
            pltpu.VMEM((NR, 8, 2, AB, RH), BF),
            pltpu.VMEM((NR, RH, K), BF),
            pltpu.VMEM((NJ, K, CJ), BF),
            pltpu.VMEM((NJ, NR, RH, CJ), jnp.int32),
            pltpu.VMEM((NR, K, RH), F32),
            pltpu.VMEM((NJ, K, CJ), F32),
            pltpu.VMEM((2, RH, CJ), BF),
            pltpu.VMEM((NJ, 7, DB, CJ), BF),
            pltpu.VMEM((NJ, 7, DB, CJ), BF),
            pltpu.VMEM((NR, 7, AB, RH), BF),
            pltpu.VMEM((NR, 7, AB, RH), BF),
            pltpu.VMEM((NR, 8, AB, RH), BF),
            pltpu.VMEM((NR, 8, AB, RH), BF),
            pltpu.SemaphoreType.DMA((2,)),
            pltpu.SemaphoreType.DMA((N_SEM,)),
            pltpu.SemaphoreType.DMA((NJ * NR,)),
        ],
        compiler_params=pltpu.CompilerParams(
            collective_id=0, has_side_effects=True, vmem_limit_bytes=60 << 20
        ),
        name="irt_step",
    )(ability.T, discrim.T, difficulty[None, :], response)
    ability_new, ability_m_new, ability_v_new = adam_update(ability, ability_m, ability_v, ga_t.T, 0.05)
    discrim_new, discrim_m_new, discrim_v_new = adam_update(discrim, discrim_m, discrim_v, gd_t.T, 0.01)
    return (ability_new, ability_m_new, ability_v_new, discrim_new, discrim_m_new, discrim_v_new)


def solution(mesh):
    return jax.shard_map(
        shards,
        mesh=mesh,
        in_specs=(
            P("mp", "item"),
            P("item"),
            P("mp", "item"),
            P("mp", "item"),
            P("mp", "item"),
            P("item", "mp"),
            P("item", "mp"),
            P("item", "mp"),
        ),
        out_specs=(
            P("mp", "item"),
            P("mp", "item"),
            P("mp", "item"),
            P("item", "mp"),
            P("item", "mp"),
            P("item", "mp"),
        ),
        check_vma=False,
    )
```

```python
import math

import jax
import jax.numpy as jnp
from jax import lax
from jax.experimental import pallas as pl
from jax.experimental.pallas import tpu as pltpu
from jax.sharding import PartitionSpec as P

K = 256
N = 2048
ROWS = (512, 1024, 512)
COLS = (256, 768, 768, 256)
NR, NJ = len(ROWS), len(COLS)
ROW_AT = tuple(sum(ROWS[:r]) for r in range(NR))
COL_AT = tuple(sum(COLS[:j]) for j in range(NJ))
RING = 4
DB, AB = 32, 16
UNIT = 8 * 256 * 4

TILES = ((1, 0), (0, 0), (0, 1), (1, 1), (2, 1), (3, 1), (1, 2), (3, 0), (3, 2), (2, 0), (2, 2), (0, 2))

G_D, G_A, S_D, S_A = 0, 3 * NJ, 3 * NJ + 3 * NR, 6 * NJ + 3 * NR
N_SEM = 6 * NJ + 6 * NR
L_IN, L_OUT_A, L_OUT_D, L_RESP = 0, 3, 3 + NR, 3 + NR + NJ
N_LOCAL = 3 + NR + NJ + NR * NJ

beta_one = 0.9
beta_two = 0.999
corr_one = 1.0 - 0.9**10
corr_two = 1.0 - 0.999**10
adam_eps = 1e-08

BF = jnp.bfloat16
F32 = jnp.float32


def adam_update(factor, moment, second, gradient, step_rate):
    moment_new = beta_one * moment + (1.0 - beta_one) * gradient
    second_new = beta_two * second + (1.0 - beta_two) * gradient * gradient
    update = moment_new / corr_one / (jnp.sqrt(second_new / corr_two) + adam_eps)
    return (factor - step_rate * update, moment_new, second_new)


def kernel(ability_hbm, discrim_hbm, diff_hbm, resp_hbm, ga_hbm, gd_hbm, *scratch):
    scratch = list(scratch)

    def take(n):
        taken, scratch[:n] = scratch[:n], []
        return taken

    at, asc, ga, sa, ra, cs, cr = (take(NR) for _ in range(7))
    dt, gd, sd, rd = (take(NJ) for _ in range(4))
    rv, ability_ref, discrim_ref, diff_ref, ga_out, gd_out = take(6)
    rb = take(2)
    send_sem, recv_sem, local_sem = scratch

    mp, item = lax.axis_index("mp"), lax.axis_index("item")
    x, p = mp // 2, mp % 2
    z, y, c = item // 8, (item // 2) % RING, item % 2

    def mp_dev(dx, flip):
        return {"mp": ((x + dx) % RING) * 2 + (1 - p if flip else p)}

    def item_dev(dy, flip):
        return {"item": ((1 - z if flip else z) * RING + (y + dy) % RING) * 2 + c}

    xs = {d: mp_dev(d, False) for d in (1, 2, 3)}
    ys = {d: item_dev(d, False) for d in (1, 2, 3)}
    x_pair, y_pair = mp_dev(0, True), item_dev(0, True)
    core = {"item": item + 1 - 2 * c}

    sent_rows = [0, 0]

    def send(phase, index, src, dst, device):
        pltpu.make_async_remote_copy(
            src_ref=src, dst_ref=dst, send_sem=send_sem.at[phase], recv_sem=recv_sem.at[index],
            device_id=device, device_id_type=pl.DeviceIdType.MESH,
        ).start()
        sent_rows[phase] += math.prod(src.shape) * 2 // UNIT

    def wait_rows(sem, rows):
        ref = rv.at[0 : 8 * rows, 0:256]
        pltpu.make_async_copy(ref, ref, sem).wait()

    def arrive(index, blocks, block_bytes):
        wait_rows(recv_sem.at[index], blocks * block_bytes // UNIT)

    def d_rows(dx, flip):
        block = ((x + dx) % RING) * 2 + (1 - p if flip else p)
        return pl.multiple_of(block * DB, DB)

    def d_send(j, s, dx, flip, device):
        ref = dt[j].at[pl.ds(d_rows(dx, flip), DB), :]
        send(0, G_D + 3 * j + s, ref, ref, device)

    def d_step0(j):
        d_send(j, 0, 0, False, x_pair)
        d_send(j, 1, 0, False, xs[2])
        d_send(j, 2, 0, False, xs[1])
        d_send(j, 2, 0, False, xs[3])

    def d_step1(j):
        arrive(G_D + 3 * j, 1, DB * COLS[j] * 2)
        d_send(j, 2, 0, True, xs[1])
        d_send(j, 2, 0, True, xs[3])

    def d_step2(j):
        arrive(G_D + 3 * j + 1, 1, DB * COLS[j] * 2)
        d_send(j, 2, 2, False, x_pair)

    def d_done(j):
        arrive(G_D + 3 * j + 2, 5, DB * COLS[j] * 2)

    def a_chip(dy, flip):
        return (1 - z if flip else z) * RING + (y + dy) % RING

    def a_send(r, s, dy, flip, device):
        ref = at[r].at[a_chip(dy, flip), c]
        send(0, G_A + 3 * r + s, ref, ref, device)

    def a_step0(r):
        a_send(r, 0, 0, False, y_pair)
        for d in (2, 1, 3):
            a_send(r, 1, 0, False, ys[d])

    def a_step1(r):
        arrive(G_A + 3 * r, 1, AB * ROWS[r] * 2)
        for d in (2, 1, 3):
            a_send(r, 1, 0, True, ys[d])

    def a_step2(r):
        arrive(G_A + 3 * r + 1, 6, AB * ROWS[r] * 2)
        ref = at[r].at[:, c]
        send(0, G_A + 3 * r + 2, ref, ref, core)

    def a_done(r):
        arrive(G_A + 3 * r + 2, 8, AB * ROWS[r] * 2)
        for i in range(0, ROWS[r], 256):
            part = at[r][:, :, :, i : i + 256].reshape(K, 256).astype(F32) * 0.5
            asc[r][i : i + 256, :] = part.T.astype(BF)

    def rd_send(j, m, s, value, device):
        sd[j][m] = value.astype(BF)
        send(1, S_D + 3 * j + s, sd[j].at[m], rd[j].at[m], device)

    def d_part(j, dx, flip):
        return gd[j][pl.ds(d_rows(dx, flip), DB), :]

    def d_in(j, m):
        return rd[j][m].astype(F32)

    def rd_step1(j):
        rd_send(j, 0, 0, d_part(j, 1, True), xs[1])
        rd_send(j, 1, 0, d_part(j, 3, True), xs[3])
        rd_send(j, 2, 1, d_part(j, 2, True), x_pair)
        rd_send(j, 3, 2, d_part(j, 1, False), xs[1])
        rd_send(j, 4, 2, d_part(j, 3, False), xs[3])

    def rd_step2(j):
        arrive(S_D + 3 * j + 1, 1, DB * COLS[j] * 2)
        rd_send(j, 6, 2, d_part(j, 2, False) + d_in(j, 2), xs[2])
        arrive(S_D + 3 * j, 2, DB * COLS[j] * 2)
        rd_send(j, 5, 2, d_part(j, 0, True) + d_in(j, 0) + d_in(j, 1), x_pair)

    d_scale = 0.5 * math.sqrt(1.0 / 16384)
    a_scale = 0.5 * math.sqrt(K / 32768)

    def rd_final(j):
        arrive(S_D + 3 * j + 2, 4, DB * COLS[j] * 2)
        total = d_part(j, 0, False)
        for m in (3, 4, 5, 6):
            total = total + d_in(j, m)
        cols = slice(COL_AT[j], COL_AT[j] + COLS[j])
        gd_out[:, cols] = total * d_scale
        out_copy(gd_out, gd_hbm, cols, L_OUT_D + j).start()

    def a_rows(chip, which):
        return pl.ds(pl.multiple_of((chip * 2 + which) * AB, AB), AB)

    def ra_core(r):
        for b in range(8):
            cs[r][b] = ga[r][a_rows(b, 1 - c), :].astype(BF)
        send(1, S_A + 3 * r, cs[r], cr[r], core)

    def a_part(r, dy, flip):
        chip = a_chip(dy, flip)
        return ga[r][a_rows(chip, c), :] + cr[r][chip].astype(F32)

    def ra_send(r, m, s, value, device):
        sa[r][m] = value.astype(BF)
        send(1, S_A + 3 * r + s, sa[r].at[m], ra[r].at[m], device)

    def ra_step1(r):
        arrive(S_A + 3 * r, 8, AB * ROWS[r] * 2)
        for d in (2, 1, 3):
            ra_send(r, d - 1, 1, a_part(r, d, True), ys[d])
        for d in (2, 1, 3):
            ra_send(r, d + 2, 2, a_part(r, d, False), ys[d])

    def ra_step2(r):
        arrive(S_A + 3 * r + 1, 3, AB * ROWS[r] * 2)
        total = a_part(r, 0, True)
        for m in (0, 1, 2):
            total = total + ra[r][m].astype(F32)
        ra_send(r, 6, 2, total, y_pair)

    def ra_final(r):
        arrive(S_A + 3 * r + 2, 4, AB * ROWS[r] * 2)
        total = a_part(r, 0, False)
        for m in (3, 4, 5, 6):
            total = total + ra[r][m].astype(F32)
        cols = slice(ROW_AT[r], ROW_AT[r] + ROWS[r])
        ga_out[:, cols] = total * a_scale
        out_copy(ga_out, ga_hbm, cols, L_OUT_A + r).start()

    def resp_copy(j, r):
        rows, cols = slice(ROW_AT[r], ROW_AT[r] + ROWS[r]), slice(COL_AT[j], COL_AT[j] + COLS[j])
        return pltpu.make_async_copy(
            resp_hbm.at[rows, cols], rv.at[rows, cols], local_sem.at[L_RESP + j * NR + r]
        )

    def residual_of(t):
        j, r = TILES[t]
        return rb[t % 2].at[0 : ROWS[r], 0 : COLS[j]]

    def front(t):
        j, r = TILES[t]
        rows, cols = slice(ROW_AT[r], ROW_AT[r] + ROWS[r]), slice(COL_AT[j], COL_AT[j] + COLS[j])
        resp_copy(j, r).wait()
        logits = jnp.dot(asc[r][...], dt[j][...], preferred_element_type=F32) + diff_ref[:, cols] * 0.5
        score = rv[rows, cols]
        sign = jnp.where(score == 2, -1.0, 1.0)
        residual_of(t)[...] = jnp.where(score > 0, jnp.tanh(logits) + sign, 0.0).astype(BF)

    seen_j, seen_r = set(), set()

    def back(t):
        j, r = TILES[t]
        residual = residual_of(t)[...]
        part_a = lax.dot_general(dt[j][...], residual, (((1,), (1,)), ((), ())), preferred_element_type=F32)
        part_d = jnp.dot(at[r][...].reshape(K, ROWS[r]), residual, preferred_element_type=F32)
        if r in seen_r:
            ga[r][...] += part_a
        else:
            ga[r][...] = part_a
        if j in seen_j:
            gd[j][...] += part_d
        else:
            gd[j][...] = part_d
        seen_r.add(r)
        seen_j.add(j)

    def out_copy(src, dst, cols, index):
        return pltpu.make_async_copy(src.at[:, cols], dst.at[:, cols], local_sem.at[index])

    barrier = pltpu.get_barrier_semaphore()
    neighbours = (*xs.values(), x_pair, *ys.values(), y_pair, core)
    for device in neighbours:
        pl.semaphore_signal(barrier, inc=1, device_id=device, device_id_type=pl.DeviceIdType.MESH)

    inputs = [
        pltpu.make_async_copy(src, dst, local_sem.at[L_IN + i])
        for i, (src, dst) in enumerate(
            ((discrim_hbm, discrim_ref), (ability_hbm, ability_ref), (diff_hbm, diff_ref))
        )
    ]
    for copy in inputs:
        copy.start()
    for j, r in TILES:
        resp_copy(j, r).start()
    for copy in inputs:
        copy.wait()
    for r in range(NR):
        at[r][a_chip(0, False), c] = ability_ref[:, ROW_AT[r] : ROW_AT[r] + ROWS[r]].astype(BF)
    for j in range(NJ):
        dt[j][pl.ds(d_rows(0, False), DB), :] = discrim_ref[:, COL_AT[j] : COL_AT[j] + COLS[j]].astype(BF)
    pl.semaphore_wait(barrier, len(neighbours))

    a_step0(0)
    d_step0(0)
    a_step0(1)
    d_step0(1)
    a_step0(2)
    d_step0(2)
    d_step1(0)
    a_step1(0)
    d_step2(0)
    a_step1(1)
    d_step1(1)
    d_step2(1)
    a_step1(2)
    d_step0(3)
    d_step1(2)
    a_step2(0)
    d_step2(2)
    a_done(0)
    a_step2(1)
    d_step1(3)
    d_done(1)
    front(0)
    d_done(0)
    front(1)
    back(0)
    a_step2(2)
    a_done(1)
    d_step2(3)
    front(2)
    back(1)
    front(3)
    back(2)
    d_done(2)
    front(4)
    back(3)
    d_done(3)
    front(5)
    back(4)
    a_done(2)
    front(6)
    back(5)
    ra_core(1)
    front(7)
    back(6)
    rd_step1(1)
    front(8)
    back(7)
    front(9)
    back(8)
    ra_step1(1)
    rd_step1(3)
    front(10)
    back(9)
    ra_core(0)
    front(11)
    back(10)
    rd_step1(2)
    back(11)
    ra_core(2)
    rd_step1(0)
    rd_step2(1)
    ra_step1(0)
    ra_step1(2)
    ra_step2(1)
    rd_step2(3)
    rd_step2(2)
    ra_step2(0)
    rd_step2(0)
    ra_step2(2)
    ra_final(1)
    rd_final(1)
    rd_final(3)
    ra_final(0)
    rd_final(2)
    rd_final(0)
    ra_final(2)
    for phase in range(2):
        wait_rows(send_sem.at[phase], sent_rows[phase])
    for r in range(NR):
        out_copy(ga_out, ga_hbm, slice(ROW_AT[r], ROW_AT[r] + ROWS[r]), L_OUT_A + r).wait()
    for j in range(NJ):
        out_copy(gd_out, gd_hbm, slice(COL_AT[j], COL_AT[j] + COLS[j]), L_OUT_D + j).wait()


def adam_kernel(ga, a, am, av, gd, d, dm, dv, a_out, am_out, av_out, d_out, dm_out, dv_out):
    for grad, old, new, step_rate in (
        (ga, (a, am, av), (a_out, am_out, av_out), 0.05),
        (gd, (d, dm, dv), (d_out, dm_out, dv_out), 0.01),
    ):
        values = adam_update(old[0][...], old[1][...], old[2][...], grad[...], step_rate)
        for ref, value in zip(new, values):
            ref[...] = value


def shards(response, difficulty, ability, ability_m, ability_v, discrim, discrim_m, discrim_v):
    vmem = pl.BlockSpec(memory_space=pltpu.VMEM)
    hbm = pl.BlockSpec(memory_space=pl.ANY)
    grad_shapes = (jax.ShapeDtypeStruct((AB, N), F32), jax.ShapeDtypeStruct((DB, N), F32))
    ga_t, gd_t = pl.pallas_call(
        kernel,
        out_shape=grad_shapes,
        in_specs=[hbm] * 4,
        out_specs=(hbm, hbm),
        scratch_shapes=[
            *(pltpu.VMEM((8, 2, AB, h), BF) for h in ROWS),
            *(pltpu.VMEM((h, K), BF) for h in ROWS),
            *(pltpu.VMEM((K, h), F32) for h in ROWS),
            *(pltpu.VMEM((7, AB, h), BF) for h in ROWS),
            *(pltpu.VMEM((7, AB, h), BF) for h in ROWS),
            *(pltpu.VMEM((8, AB, h), BF) for h in ROWS),
            *(pltpu.VMEM((8, AB, h), BF) for h in ROWS),
            *(pltpu.VMEM((K, w), BF) for w in COLS),
            *(pltpu.VMEM((K, w), F32) for w in COLS),
            *(pltpu.VMEM((7, DB, w), BF) for w in COLS),
            *(pltpu.VMEM((7, DB, w), BF) for w in COLS),
            pltpu.VMEM((N, N), jnp.int32),
            pltpu.VMEM((AB, N), F32),
            pltpu.VMEM((DB, N), F32),
            pltpu.VMEM((1, N), F32),
            pltpu.VMEM((AB, N), F32),
            pltpu.VMEM((DB, N), F32),
            *(pltpu.VMEM((max(ROWS), max(COLS)), BF) for _ in range(2)),
            pltpu.SemaphoreType.DMA((2,)),
            pltpu.SemaphoreType.DMA((N_SEM,)),
            pltpu.SemaphoreType.DMA((N_LOCAL,)),
        ],
        compiler_params=pltpu.CompilerParams(
            collective_id=0, has_side_effects=True, vmem_limit_bytes=60 << 20
        ),
        name="irt_step",
    )(ability.T, discrim.T, difficulty[None, :], response)
    outs = pl.pallas_call(
        adam_kernel,
        out_shape=(grad_shapes[0],) * 3 + (grad_shapes[1],) * 3,
        in_specs=[vmem] * 8,
        out_specs=(vmem,) * 6,
        name="irt_adam",
    )(ga_t, ability.T, ability_m.T, ability_v.T, gd_t, discrim.T, discrim_m.T, discrim_v.T)
    return tuple(out.T for out in outs)


def solution(mesh):
    return jax.shard_map(
        shards,
        mesh=mesh,
        in_specs=(
            P("mp", "item"),
            P("item"),
            P("mp", "item"),
            P("mp", "item"),
            P("mp", "item"),
            P("item", "mp"),
            P("item", "mp"),
            P("item", "mp"),
        ),
        out_specs=(
            P("mp", "item"),
            P("mp", "item"),
            P("mp", "item"),
            P("item", "mp"),
            P("item", "mp"),
            P("item", "mp"),
        ),
        check_vma=False,
    )
```
